128 devices in a mesh: dom: 8 (over y, core), spec: 16 (over x, z).
Axes of the slice: x: 4, y: 4, z: 4, core: 2. Of those that a mesh axis runs over, the one named last changes fastest.
Arguments:
- spectrum: float32 [256, 524288], P('spec', 'dom'), may hold values from -6 to 6
- conductance: float32 [256, 524288], P(None, ('dom', 'spec')), may hold values from 0.05 to 2
- capacitance: float32 [256, 524288], P(None, ('dom', 'spec')), may hold values from 0.05 to 2
- block_cond: float32 [4096, 128, 128], P(('dom', 'spec')), may hold values from -0.5 to 0.5
- block_cap: float32 [4096, 128, 128], P(('dom', 'spec')), may hold values from -0.5 to 0.5
- boundary_nodes: int32 [8, 256], P('dom'), may hold values from 0 to 65535, as said below
- couple_src: int32 [8, 7], P('dom'), may hold values from 0 to 7, as said below
- couple_count: int32 [8], P('dom'), may hold values from 1 to 7, as said below
- couple_cond: float32 [8, 7, 256, 256], P('dom'), may hold values from -0.375 to 0.375
- couple_cap: float32 [8, 7, 256, 256], P('dom'), may hold values from -0.375 to 0.375
Outputs:
- jacobian_product: float32 [256, 524288], P('spec', 'dom')
The draws below stay inside these ranges and needn't reach their ends.
Inputs may be any that keep to these rules, and one draw needn't show every extreme that they name: `boundary_nodes`: row d lists 256 distinct nodes of partition d; entries 16 * s to 16 * (s + 1) - 1 lie among nodes 4096 * s to 4096 * (s + 1) - 1 and increase. `couple_src`: row d holds every partition other than d once. Partition d uses the first couple_count[d] entries of its rows of couple_src, couple_cond and couple_cap; some partition uses all 7.
All inputs are finite; a program needn't handle non-finite values.
Results may differ from the reference program's by a relative error of at most 0.0001.
Values sent between devices are 32-bit elements; how exact they have to be, the bound alone decides.
No kernel may reach another device: no remote copies, remote signals or barrier semaphores. Data moves between devices by JAX's collectives and lax.ppermute only.
A program may use at most 192 MiB of HBM per device.

```python
import math
import jax
import jax.numpy as jnp
from jax import lax

S = 256
BS = 128
ND = 4096
BPD = 16
NP = 65536
NODES = 524288
NBLK = 4096
NBND = 256
MAXC = 7
N_DOM = 8


def draw_boundary_nodes(key, part):
    slices = NBND // BPD
    key_list = jax.random.split(key, N_DOM * slices)

    def pick_nodes(one_key):
        return jnp.sort(jax.random.permutation(one_key, ND)[:BPD])
    picked = jax.vmap(pick_nodes)(key_list).astype(jnp.int32)
    offsets = jnp.arange(N_DOM * slices, dtype=jnp.int32) % slices * ND
    return (picked + offsets[:, None]).reshape(N_DOM, NBND).astype(jnp.int32)


def draw_couple_src(key, part):
    key_list = jax.random.split(key, N_DOM)

    def one_row(one_key, owner_id):
        shuffled = jax.random.permutation(one_key, MAXC).astype(jnp.int32)
        return shuffled + (shuffled >= owner_id).astype(jnp.int32)
    return jax.vmap(one_row)(key_list, jnp.arange(N_DOM, dtype=jnp.int32)).astype(jnp.int32)


def draw_couple_count(key, part):
    counts = jax.random.randint(key, (N_DOM,), 1, MAXC + 1)
    fullest = jax.random.randint(jax.random.fold_in(key, 7), (), 0, N_DOM)
    return counts.at[fullest].set(MAXC).astype(jnp.int32)


def block_scale(stream_key, dims, cuts, smallest, top_value):
    def one(position, blocks):
        steps = jax.random.uniform(jax.random.fold_in(jax.random.fold_in(stream_key, 6), position), (blocks,), jnp.float32, smallest / len(cuts), top_value / len(cuts))
        return jnp.repeat(jnp.exp(steps), dims[position] // blocks).reshape((-1,) + (1,) * (len(dims) - position - 1))

    gain = one(*cuts[0])
    for cut in cuts[1:]:
        gain = gain * one(*cut)
    return gain


def bell_draw(own_key, shape, scale, reach, cuts=(), held_as=jnp.bfloat16):
    values = jax.random.normal(own_key, shape, jnp.float32) * scale
    if len(cuts) > 0:
        values = block_scale(own_key, shape, cuts, -0.22, 0.18) * values
    return jnp.clip(values, min=-reach, max=reach).astype(held_as)


def setup_inputs(seed: int = 0) -> dict:
    seeds = jax.random.split(jax.random.key(seed), 11)
    spectrum = bell_draw(seeds[0], (S, NODES), 1.0, 6.0, ((0, 16), (1, 8)), jnp.float32)
    conductance = jnp.clip(jnp.exp(math.log(2.0) - 3.6888794 * jax.random.uniform(seeds[1], (S, NODES), jnp.float32) ** block_scale(seeds[1], (S, NODES), ((1, 128),), -0.2, 0.2)), 0.05, 2.0)
    capacitance = jnp.clip(jnp.exp(math.log(2.0) - 3.6888794 * jax.random.uniform(seeds[2], (S, NODES), jnp.float32) ** block_scale(seeds[2], (S, NODES), ((1, 128),), -0.2, 0.2)), 0.05, 2.0)
    block_cond = bell_draw(seeds[3], (NBLK, BS, BS), BS ** -0.5, 0.5, ((0, 128),), jnp.float32)
    block_cap = bell_draw(seeds[4], (NBLK, BS, BS), BS ** -0.5, 0.5, ((0, 128),), jnp.float32)
    boundary_nodes = draw_boundary_nodes(jax.random.fold_in(seeds[10], 71), 0)
    couple_src = draw_couple_src(jax.random.fold_in(seeds[10], 71), 0)
    couple_count = draw_couple_count(jax.random.fold_in(seeds[10], 71), 0)
    couple_cond = bell_draw(seeds[8], (N_DOM, MAXC, NBND, NBND), NBND ** -0.5, 0.375, ((0, 8),), jnp.float32)
    couple_cap = bell_draw(seeds[9], (N_DOM, MAXC, NBND, NBND), NBND ** -0.5, 0.375, ((0, 8),), jnp.float32)
    return dict(spectrum=spectrum, conductance=conductance, capacitance=capacitance, block_cond=block_cond, block_cap=block_cap, boundary_nodes=boundary_nodes, couple_src=couple_src, couple_count=couple_count, couple_cond=couple_cond, couple_cap=couple_cap)


HIGHEST = lax.Precision.HIGHEST


def fourier_tables(length):
    time_ids = jnp.arange(length, dtype=jnp.int32)
    column_ids = jnp.arange(length, dtype=jnp.int32)
    harmonic = jnp.where(column_ids == 1, length // 2, column_ids // 2)
    phase_ids = (time_ids[:, None] * harmonic[None, :]) % length
    angles = phase_ids.astype(jnp.float32) * jnp.float32(2.0 * math.pi / length)
    is_sine = (column_ids % 2 == 1) & (column_ids >= 2)
    basis_table = jnp.where(is_sine[None, :], jnp.sin(angles), jnp.cos(angles))
    row_scale = jnp.where(column_ids < 2, 1.0 / length, 2.0 / length).astype(jnp.float32)
    forward = basis_table.T * row_scale[:, None]
    return basis_table, forward


def derivative(spectra_in, first_row, length):
    row_count = spectra_in.shape[0]
    paired = spectra_in.reshape((row_count // 2, 2) + spectra_in.shape[1:])
    pair_ids = first_row // 2 + jnp.arange(row_count // 2, dtype=jnp.int32)
    frequency = jnp.where(pair_ids >= 1, pair_ids.astype(jnp.float32) * (2.0 / length), 0.0).astype(jnp.float32)
    frequency = frequency.reshape((row_count // 2,) + (1,) * (spectra_in.ndim - 1))
    even_part = paired[:, 0]
    odd_part = paired[:, 1]
    return jnp.stack([frequency * odd_part, -frequency * even_part], axis=1).reshape(spectra_in.shape)


def network(spectra_in, slopes, block_cond, block_cap):
    length, node_count = spectra_in.shape
    block_size = block_cond.shape[1]
    shaped = spectra_in.reshape(length, node_count // block_size, block_size)
    shaped_slope = slopes.reshape(length, node_count // block_size, block_size)
    result = jnp.einsum('mbj,bij->mbi', shaped, block_cond, precision=HIGHEST)
    result = result + jnp.einsum('mbj,bij->mbi', shaped_slope, block_cap, precision=HIGHEST)
    return result.reshape(length, node_count)


def couple(gathered, first_row, length, sources, used, rows_cond, rows_cap):
    slopes = derivative(gathered, first_row, length)
    owners = jnp.arange(gathered.shape[1], dtype=jnp.int32)
    slot_ids = jnp.arange(sources.shape[0], dtype=jnp.int32)
    chosen = ((sources[:, None] == owners[None, :]) & (slot_ids < used)[:, None]).astype(jnp.float32)
    source_values = jnp.einsum('cp,mpk->cmk', chosen, gathered, precision=HIGHEST)
    source_slopes = jnp.einsum('cp,mpk->cmk', chosen, slopes, precision=HIGHEST)
    current = jnp.einsum('cmk,cjk->mj', source_values, rows_cond, precision=HIGHEST)
    return current + jnp.einsum('cmk,cjk->mj', source_slopes, rows_cap, precision=HIGHEST)


def reference(spectrum, conductance, capacitance, block_cond, block_cap, boundary_nodes, couple_src, couple_count, couple_cond, couple_cap):
    basis_table, forward = fourier_tables(S)
    waveforms = jnp.dot(basis_table, spectrum, precision=HIGHEST)
    device_current = jnp.dot(forward, conductance * waveforms, precision=HIGHEST)
    device_current = device_current + derivative(jnp.dot(forward, capacitance * waveforms, precision=HIGHEST), 0, S)
    slope_spec = derivative(spectrum, 0, S)
    summed = device_current + network(spectrum, slope_spec, block_cond, block_cap)
    partitions_view = spectrum.reshape(S, N_DOM, NP)
    bound_spec = partitions_view[:, jnp.arange(N_DOM, dtype=jnp.int32)[:, None], boundary_nodes]
    summed = summed.reshape(S, N_DOM, NP)
    for partition in range(N_DOM):
        current = couple(bound_spec, 0, S, couple_src[partition], couple_count[partition], couple_cond[partition], couple_cap[partition])
        summed = summed.at[:, partition, boundary_nodes[partition]].add(current)
    return summed.reshape(S, NODES)
```

```python
import functools
import math

import jax
import jax.numpy as jnp
import numpy as np
from jax import lax
from jax.experimental import pallas as pl
from jax.experimental.pallas import tpu as pltpu
from jax.sharding import PartitionSpec as P

F32 = jnp.float32
BF16 = jnp.bfloat16
PARTS = 2
TILE = 512


def fourier_tables(length):
    harmonic = np.arange(length) // 2
    harmonic[1] = length // 2
    phase = np.arange(length)[:, None] * harmonic[None, :] % length
    angles = phase * (2.0 * math.pi / length)
    is_sine = (np.arange(length) % 2 == 1) & (np.arange(length) >= 2)
    basis = np.where(is_sine[None, :], np.sin(angles), np.cos(angles))
    scale = np.where(np.arange(length) < 2, 1.0 / length, 2.0 / length)
    return basis.astype(np.float32), (basis.T * scale[:, None]).astype(np.float32)


def widened(table):
    high = table.astype(jnp.bfloat16)
    low = (table - high.astype(np.float32)).astype(jnp.bfloat16)
    return jnp.asarray(np.concatenate([high, high, low], axis=1))


def halves(x):
    high = x.astype(BF16)
    return high, (x - high.astype(F32)).astype(BF16)


def derive(x, first_row, length):
    rows = lax.broadcasted_iota(jnp.int32, x.shape, 0)
    up = pltpu.roll(x, x.shape[0] - 1, 0)
    down = pltpu.roll(x, 1, 0)
    freq = ((rows + first_row) // 2).astype(F32) * (2.0 / length)
    return freq * jnp.where(rows % 2 == 0, up, -down)


def nodal_kernel(length, block, s_ref, g_ref, c_ref, cond_ref, cap_ref, basis_ref, forward_ref, o_ref):
    s_high, s_low = halves(s_ref[...])
    waves = jnp.dot(
        basis_ref[...],
        jnp.concatenate([s_high, s_low, s_high], axis=0),
        preferred_element_type=F32,
    )

    def onward(values):
        high, low = halves(values)
        return jnp.dot(
            forward_ref[...],
            jnp.concatenate([high, low, high], axis=0),
            preferred_element_type=F32,
        )

    direct = onward(g_ref[...] * waves)
    stored = onward(c_ref[...] * waves)
    direct_net = []
    stored_net = []
    for b in range(cond_ref.shape[0]):
        cond_high, cond_low = halves(cond_ref[b])
        cap_high, cap_low = halves(cap_ref[b])
        left = jnp.concatenate(
            [
                s_high[:, b * block : (b + 1) * block],
                s_low[:, b * block : (b + 1) * block],
                s_high[:, b * block : (b + 1) * block],
            ],
            axis=1,
        )
        right = jnp.concatenate(
            [
                jnp.concatenate([cond_high, cond_high, cond_low], axis=1),
                jnp.concatenate([cap_high, cap_high, cap_low], axis=1),
            ],
            axis=0,
        )
        both = lax.dot_general(
            left, right, (((1,), (1,)), ((), ())), preferred_element_type=F32
        )
        direct_net.append(both[:, :block])
        stored_net.append(both[:, block:])
    direct = direct + jnp.concatenate(direct_net, axis=1)
    stored = stored + jnp.concatenate(stored_net, axis=1)
    o_ref[...] = direct + derive(stored, 0, length)


def nodal(part, s, conductance, capacitance, block_cond, block_cap, basis, forward):
    length, width = s.shape
    block = block_cond.shape[1]
    steps = width // TILE
    per = TILE // block
    column = lambda i: (0, part * steps + i)
    blocks = pl.BlockSpec((per, block, block), lambda i: (part * steps + i, 0, 0))
    table = pl.BlockSpec((length, 3 * length), lambda i: (0, 0))
    return pl.pallas_call(
        functools.partial(nodal_kernel, length, block),
        grid=(steps,),
        in_specs=[
            pl.BlockSpec((length, TILE), lambda i: (0, i)),
            pl.BlockSpec((length, TILE), column),
            pl.BlockSpec((length, TILE), column),
            blocks,
            blocks,
            table,
            table,
        ],
        out_specs=pl.BlockSpec((length, TILE), lambda i: (0, i)),
        out_shape=jax.ShapeDtypeStruct(s.shape, F32),
        compiler_params=pltpu.CompilerParams(vmem_limit_bytes=48 << 20),
        cost_estimate=pl.CostEstimate(
            flops=24 * length * length * width, transcendentals=0, bytes_accessed=20 * length * width
        ),
        name="nodal",
    )(s, conductance, capacitance, block_cond, block_cap, basis, forward)


def pack_kernel(offset, stride, x_ref, o_ref, sem):
    count, _, width = o_ref.shape
    copies = [
        pltpu.make_async_copy(
            x_ref.at[:, pl.ds(t * stride + offset, width)], o_ref.at[t], sem.at[t]
        )
        for t in range(count)
    ]
    for copy in copies:
        copy.start()
    for copy in copies:
        copy.wait()


def pack(x, part, count):
    rows, columns = x.shape
    stride = columns // count
    width = stride // PARTS
    return pl.pallas_call(
        functools.partial(pack_kernel, part * width, stride),
        in_specs=[pl.BlockSpec(memory_space=pl.ANY)],
        out_specs=pl.BlockSpec(memory_space=pl.ANY),
        out_shape=jax.ShapeDtypeStruct((count, rows, width), F32),
        scratch_shapes=[pltpu.SemaphoreType.DMA((count,))],
        name="pack",
    )(x)


def pick_kernel(per, nodes_ref, x_ref, o_ref):
    t = pl.program_id(0)
    width = x_ref.shape[1]
    lanes = lax.broadcasted_iota(jnp.int32, (x_ref.shape[0], 128), 1)
    total = jnp.zeros((x_ref.shape[0], 128), F32)
    for j in range(per):
        place = jnp.clip(nodes_ref[t * per + j] - t * width, 0, width - 1)
        tile = x_ref[:, pl.ds(pl.multiple_of(place // 128 * 128, 128), 128)]
        turned = pltpu.roll(tile, (j - place % 128 + 128) % 128, 1)
        total = jnp.where(lanes == j, turned, total)
    o_ref[...] = total


def pick(x, nodes, count):
    rows, columns = x.shape
    per = nodes.shape[0] // count
    picked = pl.pallas_call(
        functools.partial(pick_kernel, per),
        grid_spec=pltpu.PrefetchScalarGridSpec(
            num_scalar_prefetch=1,
            grid=(count,),
            in_specs=[pl.BlockSpec((rows, columns // count), lambda t, n: (0, t))],
            out_specs=pl.BlockSpec((None, rows, 128), lambda t, n: (t, 0, 0)),
        ),
        out_shape=jax.ShapeDtypeStruct((count, rows, 128), F32),
        name="pick",
    )(nodes, x)
    return picked[:, :, :per].transpose(1, 0, 2).reshape(rows, nodes.shape[0])


def couple_kernel(length, scalars_ref, x_ref, cond_ref, cap_ref, o_ref):
    c = pl.program_id(0)

    @pl.when(c == 0)
    def _():
        o_ref[...] = jnp.zeros_like(o_ref)

    @pl.when(c < scalars_ref[0])
    def _():
        x = x_ref[...]
        slope = derive(x, scalars_ref[1], length)

        def times(left, right):
            left_high, left_low = halves(left)
            right_high, right_low = halves(right)
            contract = (((1,), (1,)), ((), ()))
            product = functools.partial(
                lax.dot_general, dimension_numbers=contract, preferred_element_type=F32
            )
            return (
                product(left_high, right_high)
                + product(left_low, right_high)
                + product(left_high, right_low)
            )

        o_ref[...] += times(x, cond_ref[...]) + times(slope, cap_ref[...])


def couple(gathered, sources, used, first_row, length, couple_cond, couple_cap):
    _, rows, bound = gathered.shape
    slots = sources.shape[0]
    scalars = jnp.concatenate([used, first_row[None], sources])
    table = pl.BlockSpec((None, None, bound, bound), lambda c, n: (0, c, 0, 0))
    return pl.pallas_call(
        functools.partial(couple_kernel, length),
        grid_spec=pltpu.PrefetchScalarGridSpec(
            num_scalar_prefetch=1,
            grid=(slots,),
            in_specs=[
                pl.BlockSpec((None, rows, bound), lambda c, n: (n[2 + c], 0, 0)),
                table,
                table,
            ],
            out_specs=pl.BlockSpec((rows, bound), lambda c, n: (0, 0)),
        ),
        out_shape=jax.ShapeDtypeStruct((rows, bound), F32),
        name="couple",
    )(scalars, gathered, couple_cond, couple_cap)


def place_kernel(part, stride, group, nodes_ref, y_ref, extra_ref, *rest):
    o_ref = rest[-1]
    step = pl.program_id(0)
    _, rows, width = y_ref.shape
    per = extra_ref.shape[2]
    lanes = lax.broadcasted_iota(jnp.int32, (rows, 128), 1)
    for g in range(group):
        t = step * group + g
        lo = g * stride + part * width
        o_ref[:, g * width : (g + 1) * width] = y_ref[g]
        extra = extra_ref[g]
        for j in range(per):
            local = nodes_ref[t * per + j] - t * stride - part * width
            first = jnp.clip(local // 128, 0, width // 128 - 1) * 128
            at = pl.ds(pl.multiple_of(g * width + first, 128), 128)
            old = o_ref[:, at]
            o_ref[:, at] = old + jnp.where(lanes + first == local, extra[:, j : j + 1], 0.0)


def place(y, extra, nodes, part, held):
    count, rows, width = y.shape
    per = nodes.shape[0] // count
    stride = width * PARTS
    in_specs = [
        pl.BlockSpec((1, rows, width), lambda t, n: (t, 0, 0)),
        pl.BlockSpec((1, rows, per), lambda t, n: (t, 0, 0)),
    ]
    args = [y, extra]
    aliases = {}
    if held is not None:
        in_specs.append(pl.BlockSpec(memory_space=pl.ANY))
        args.append(held)
        aliases = {3: 0}
    return pl.pallas_call(
        functools.partial(place_kernel, part, stride, 1),
        grid_spec=pltpu.PrefetchScalarGridSpec(
            num_scalar_prefetch=1,
            grid=(count,),
            in_specs=in_specs,
            out_specs=pl.BlockSpec((rows, width), lambda t, n: (0, t * PARTS + part)),
        ),
        out_shape=jax.ShapeDtypeStruct((rows, count * stride), F32),
        input_output_aliases=aliases,
        name="place",
    )(nodes, *args)


def shards(
    spectrum,
    conductance,
    capacitance,
    block_cond,
    block_cap,
    boundary_nodes,
    couple_src,
    couple_count,
    couple_cond,
    couple_cap,
):
    length = conductance.shape[0]
    rows = spectrum.shape[0]
    count = lax.axis_size("spec")
    basis_table, forward_table = fourier_tables(length)
    basis, forward = widened(basis_table), widened(forward_table)
    nodes = boundary_nodes[0]
    nodal_args = (conductance, capacitance, block_cond, block_cap, basis, forward)

    def swap(x):
        return lax.all_to_all(x, "spec", split_axis=0, concat_axis=0, tiled=True)

    arrived = []
    for part in range(PARTS):
        got = swap(pack(spectrum, part, count))
        arrived.append(got.reshape(length, got.shape[2]))

    own_boundary = pick(spectrum, nodes, count)
    gathered = lax.all_gather(own_boundary, "dom", axis=0, tiled=False)
    extra = couple(
        gathered,
        couple_src[0],
        couple_count,
        lax.axis_index("spec") * rows,
        length,
        couple_cond,
        couple_cap,
    )
    extra = extra.reshape(rows, count, nodes.shape[0] // count).transpose(1, 0, 2)

    result = None
    for part in range(PARTS):
        current = nodal(part, arrived[part], *nodal_args)
        back = swap(current.reshape(count, rows, current.shape[1]))
        result = place(back, extra, nodes, part, result)
    return result


def solution(mesh):
    return jax.shard_map(
        shards,
        mesh=mesh,
        in_specs=(
            P("spec", "dom"),
            P(None, ("dom", "spec")),
            P(None, ("dom", "spec")),
            P(("dom", "spec"), None, None),
            P(("dom", "spec"), None, None),
            P("dom", None),
            P("dom", None),
            P("dom"),
            P("dom", None, None, None),
            P("dom", None, None, None),
        ),
        out_specs=P("spec", "dom"),
        check_vma=False,
    )
```

```python
import functools
import math

import jax
import jax.numpy as jnp
import numpy as np
from jax import lax
from jax.experimental import pallas as pl
from jax.experimental.pallas import tpu as pltpu
from jax.sharding import PartitionSpec as P

F32 = jnp.float32
BF16 = jnp.bfloat16
PARTS = 2
TILE = 512


def fourier_tables(length):
    harmonic = np.arange(length) // 2
    harmonic[1] = length // 2
    phase = np.arange(length)[:, None] * harmonic[None, :] % length
    angles = phase * (2.0 * math.pi / length)
    is_sine = (np.arange(length) % 2 == 1) & (np.arange(length) >= 2)
    basis = np.where(is_sine[None, :], np.sin(angles), np.cos(angles))
    scale = np.where(np.arange(length) < 2, 1.0 / length, 2.0 / length)
    return basis.astype(np.float32), (basis.T * scale[:, None]).astype(np.float32)


def widened(table):
    high = table.astype(jnp.bfloat16)
    low = (table - high.astype(np.float32)).astype(jnp.bfloat16)
    return jnp.asarray(np.concatenate([high, high, low], axis=1))


def halves(x):
    high = x.astype(BF16)
    return high, (x - high.astype(F32)).astype(BF16)


def derive(x, first_row, length):
    rows = lax.broadcasted_iota(jnp.int32, x.shape, 0)
    up = pltpu.roll(x, x.shape[0] - 1, 0)
    down = pltpu.roll(x, 1, 0)
    freq = ((rows + first_row) // 2).astype(F32) * (2.0 / length)
    return freq * jnp.where(rows % 2 == 0, up, -down)


def nodal_kernel(length, block, s_ref, g_ref, c_ref, cond_ref, cap_ref, basis_ref, forward_ref, o_ref):
    s_high, s_low = halves(s_ref[...].reshape(length, s_ref.shape[2]))
    waves = jnp.dot(
        basis_ref[...],
        jnp.concatenate([s_high, s_low, s_high], axis=0),
        preferred_element_type=F32,
    )

    def onward(values):
        high, low = halves(values)
        return jnp.dot(
            forward_ref[...],
            jnp.concatenate([high, low, high], axis=0),
            preferred_element_type=F32,
        )

    direct = onward(g_ref[...] * waves)
    stored = onward(c_ref[...] * waves)
    direct_net = []
    stored_net = []
    for b in range(cond_ref.shape[0]):
        cond_high, cond_low = halves(cond_ref[b])
        cap_high, cap_low = halves(cap_ref[b])
        left = jnp.concatenate(
            [
                s_high[:, b * block : (b + 1) * block],
                s_low[:, b * block : (b + 1) * block],
                s_high[:, b * block : (b + 1) * block],
            ],
            axis=1,
        )
        right = jnp.concatenate(
            [
                jnp.concatenate([cond_high, cond_high, cond_low], axis=1),
                jnp.concatenate([cap_high, cap_high, cap_low], axis=1),
            ],
            axis=0,
        )
        both = lax.dot_general(
            left, right, (((1,), (1,)), ((), ())), preferred_element_type=F32
        )
        direct_net.append(both[:, :block])
        stored_net.append(both[:, block:])
    direct = direct + jnp.concatenate(direct_net, axis=1)
    stored = stored + jnp.concatenate(stored_net, axis=1)
    o_ref[...] = (direct + derive(stored, 0, length)).reshape(o_ref.shape)


def nodal(part, s, conductance, capacitance, block_cond, block_cap, basis, forward):
    count, rows, width = s.shape
    length = count * rows
    block = block_cond.shape[1]
    steps = width // TILE
    per = TILE // block
    column = lambda i: (0, part * steps + i)
    blocks = pl.BlockSpec((per, block, block), lambda i: (part * steps + i, 0, 0))
    table = pl.BlockSpec((length, 3 * length), lambda i: (0, 0))
    return pl.pallas_call(
        functools.partial(nodal_kernel, length, block),
        grid=(steps,),
        in_specs=[
            pl.BlockSpec((count, rows, TILE), lambda i: (0, 0, i)),
            pl.BlockSpec((length, TILE), column),
            pl.BlockSpec((length, TILE), column),
            blocks,
            blocks,
            table,
            table,
        ],
        out_specs=pl.BlockSpec((count, rows, TILE), lambda i: (0, 0, i)),
        out_shape=jax.ShapeDtypeStruct(s.shape, F32),
        compiler_params=pltpu.CompilerParams(vmem_limit_bytes=48 << 20),
        cost_estimate=pl.CostEstimate(
            flops=24 * length * length * width, transcendentals=0, bytes_accessed=20 * length * width
        ),
        name="nodal",
    )(in_hbm(s), conductance, capacitance, block_cond, block_cap, basis, forward)


def pack_kernel(offset, stride, x_ref, o_ref, held, sem_in, sem_out):
    count, _, width = o_ref.shape
    loads = [
        pltpu.make_async_copy(
            x_ref.at[:, pl.ds(t * stride + offset, width)], held.at[t], sem_in.at[t]
        )
        for t in range(count)
    ]
    stores = [
        pltpu.make_async_copy(held.at[t], o_ref.at[t], sem_out.at[t]) for t in range(count)
    ]
    for load in loads:
        load.start()
    for load, store in zip(loads, stores):
        load.wait()
        store.start()
    for store in stores:
        store.wait()


def pack(x, part, count):
    rows, columns = x.shape
    stride = columns // count
    width = stride // PARTS
    return pl.pallas_call(
        functools.partial(pack_kernel, part * width, stride),
        in_specs=[pl.BlockSpec(memory_space=pl.ANY)],
        out_specs=pl.BlockSpec(memory_space=pl.ANY),
        out_shape=jax.ShapeDtypeStruct((count, rows, width), F32),
        scratch_shapes=[
            pltpu.VMEM((count, rows, width), F32),
            pltpu.SemaphoreType.DMA((count,)),
            pltpu.SemaphoreType.DMA((count,)),
        ],
        name="pack",
    )(x)


def pick_kernel(per, nodes_ref, x_ref, o_ref):
    t = pl.program_id(0)
    lanes = lax.broadcasted_iota(jnp.int32, (x_ref.shape[0], 128), 1)
    total = jnp.zeros((x_ref.shape[0], 128), F32)
    for j in range(per):
        spot = nodes_ref[t * per + j]
        tile = x_ref[:, pl.ds(pl.multiple_of(spot & ~127, 128), 128)]
        turned = pltpu.roll(tile, (j - spot) & 127, 1)
        total = jnp.where(lanes == j, turned, total)
    o_ref[...] = total


def pick(x, nodes, count):
    rows, columns = x.shape
    per = nodes.shape[0] // count
    picked = pl.pallas_call(
        functools.partial(pick_kernel, per),
        grid_spec=pltpu.PrefetchScalarGridSpec(
            num_scalar_prefetch=1,
            grid=(count,),
            in_specs=[pl.BlockSpec((rows, columns // count), lambda t, n: (0, t))],
            out_specs=pl.BlockSpec((None, rows, 128), lambda t, n: (t, 0, 0)),
        ),
        out_shape=jax.ShapeDtypeStruct((count, rows, 128), F32),
        name="pick",
    )(nodes, x)
    return picked[:, :, :per].transpose(1, 0, 2).reshape(rows, nodes.shape[0])


def couple_kernel(length, scalars_ref, x_ref, cond_ref, cap_ref, o_ref):
    c = pl.program_id(0)

    @pl.when(c == 0)
    def _():
        o_ref[...] = jnp.zeros_like(o_ref)

    @pl.when(c < scalars_ref[0])
    def _():
        x = x_ref[...]
        slope = derive(x, scalars_ref[1], length)

        def times(left, right):
            left_high, left_low = halves(left)
            right_high, right_low = halves(right)
            contract = (((1,), (1,)), ((), ()))
            product = functools.partial(
                lax.dot_general, dimension_numbers=contract, preferred_element_type=F32
            )
            return (
                product(left_high, right_high)
                + product(left_low, right_high)
                + product(left_high, right_low)
            )

        o_ref[...] += times(x, cond_ref[...]) + times(slope, cap_ref[...])


def couple(gathered, sources, used, first_row, length, couple_cond, couple_cap):
    _, rows, bound = gathered.shape
    slots = sources.shape[0]
    scalars = jnp.concatenate([used, first_row[None], sources])
    table = pl.BlockSpec((None, None, bound, bound), lambda c, n: (0, c, 0, 0))
    return pl.pallas_call(
        functools.partial(couple_kernel, length),
        grid_spec=pltpu.PrefetchScalarGridSpec(
            num_scalar_prefetch=1,
            grid=(slots,),
            in_specs=[
                pl.BlockSpec((None, rows, bound), lambda c, n: (n[2 + c], 0, 0)),
                table,
                table,
            ],
            out_specs=pl.BlockSpec((rows, bound), lambda c, n: (0, 0)),
        ),
        out_shape=jax.ShapeDtypeStruct((rows, bound), F32),
        name="couple",
    )(scalars, gathered, couple_cond, couple_cap)


def spread_kernel(nodes_ref, extra_ref, o_ref):
    t = pl.program_id(0)
    rows = o_ref.shape[0]
    per = extra_ref.shape[1]
    lanes = lax.broadcasted_iota(jnp.int32, (rows, 128), 1)
    o_ref[...] = jnp.zeros_like(o_ref)
    extra = extra_ref[...]
    for j in range(per):
        spot = nodes_ref[t * per + j]
        at = pl.ds(pl.multiple_of(spot & ~127, 128), 128)
        o_ref[:, at] += jnp.where(lanes == (spot & 127), extra[:, j : j + 1], 0.0)


def spread(extra, nodes, width):
    count, rows, per = extra.shape
    return pl.pallas_call(
        spread_kernel,
        grid_spec=pltpu.PrefetchScalarGridSpec(
            num_scalar_prefetch=1,
            grid=(count,),
            in_specs=[pl.BlockSpec((None, rows, per), lambda t, n: (t, 0, 0))],
            out_specs=pl.BlockSpec((rows, width), lambda t, n: (0, t)),
        ),
        out_shape=jax.ShapeDtypeStruct((rows, count * width), F32),
        name="spread",
    )(nodes, extra)


def place_kernel(part, stride, y_ref, held_ref, o_ref, y_buf, held_buf, sem_y, sem_held, sem_out):
    count, _, width = y_ref.shape
    at = [pl.ds(t * stride + part * width, width) for t in range(count)]
    loads = [
        (
            pltpu.make_async_copy(y_ref.at[t], y_buf.at[t], sem_y.at[t]),
            pltpu.make_async_copy(held_ref.at[:, at[t]], held_buf.at[t], sem_held.at[t]),
        )
        for t in range(count)
    ]
    stores = [
        pltpu.make_async_copy(y_buf.at[t], o_ref.at[:, at[t]], sem_out.at[t])
        for t in range(count)
    ]
    for first, second in loads:
        first.start()
        second.start()
    for t in range(count):
        loads[t][0].wait()
        loads[t][1].wait()
        y_buf[t] = y_buf[t] + held_buf[t]
        stores[t].start()
    for store in stores:
        store.wait()


def place(y, part, held):
    count, rows, width = y.shape
    return pl.pallas_call(
        functools.partial(place_kernel, part, width * PARTS),
        in_specs=[pl.BlockSpec(memory_space=pl.ANY)] * 2,
        out_specs=pl.BlockSpec(memory_space=pl.ANY),
        out_shape=jax.ShapeDtypeStruct(held.shape, F32),
        scratch_shapes=[
            pltpu.VMEM(y.shape, F32),
            pltpu.VMEM(y.shape, F32),
            pltpu.SemaphoreType.DMA((count,)),
            pltpu.SemaphoreType.DMA((count,)),
            pltpu.SemaphoreType.DMA((count,)),
        ],
        input_output_aliases={1: 0},
        name="place",
    )(in_hbm(y), held)


def in_hbm(x):
    return pltpu.with_memory_space_constraint(x, pltpu.HBM)


def shards(
    spectrum,
    conductance,
    capacitance,
    block_cond,
    block_cap,
    boundary_nodes,
    couple_src,
    couple_count,
    couple_cond,
    couple_cap,
):
    length = conductance.shape[0]
    rows = spectrum.shape[0]
    count = lax.axis_size("spec")
    basis_table, forward_table = fourier_tables(length)
    basis, forward = widened(basis_table), widened(forward_table)
    stride = spectrum.shape[1] // count
    nodes = boundary_nodes[0]
    slices = jnp.arange(nodes.shape[0], dtype=jnp.int32) // (nodes.shape[0] // count)
    nodes = jnp.clip(nodes - slices * stride, 0, stride - 1)
    nodal_args = (conductance, capacitance, block_cond, block_cap, basis, forward)

    def swap(x):
        return lax.all_to_all(x, "spec", split_axis=0, concat_axis=0, tiled=True)

    arrived = []
    for part in range(PARTS):
        packed = pack(spectrum, part, count)
        if part == 1:
            own_boundary = pick(spectrum, nodes, count)
            gathered = lax.all_gather(own_boundary, "dom", axis=0, tiled=False)
            packed, gathered = lax.optimization_barrier((packed, gathered))
        arrived.append(swap(packed))

    extra = couple(
        gathered,
        couple_src[0],
        couple_count,
        lax.axis_index("spec") * rows,
        length,
        couple_cond,
        couple_cap,
    )
    extra = extra.reshape(rows, count, nodes.shape[0] // count).transpose(1, 0, 2)

    for part in range(PARTS):
        current = nodal(part, arrived[part], *nodal_args)
        if part == 0:
            current, extra = lax.optimization_barrier((current, extra))
            result = spread(extra, nodes, stride)
        if part == 1:
            current, result = lax.optimization_barrier((current, result))
        back = swap(current)
        result = place(back, part, result)
    return result


def solution(mesh):
    return jax.shard_map(
        shards,
        mesh=mesh,
        in_specs=(
            P("spec", "dom"),
            P(None, ("dom", "spec")),
            P(None, ("dom", "spec")),
            P(("dom", "spec"), None, None),
            P(("dom", "spec"), None, None),
            P("dom", None),
            P("dom", None),
            P("dom"),
            P("dom", None, None, None),
            P("dom", None, None, None),
        ),
        out_specs=P("spec", "dom"),
        check_vma=False,
    )
```

```python
import functools
import math

import jax
import jax.numpy as jnp
import numpy as np
from jax import lax
from jax.experimental import pallas as pl
from jax.experimental.pallas import tpu as pltpu
from jax.sharding import PartitionSpec as P

F32 = jnp.float32
BF16 = jnp.bfloat16
PARTS = 2
TILE = 512
GROUP = 4
EARLY = 4


def fourier_tables(length):
    harmonic = np.arange(length) // 2
    harmonic[1] = length // 2
    phase = np.arange(length)[:, None] * harmonic[None, :] % length
    angles = phase * (2.0 * math.pi / length)
    is_sine = (np.arange(length) % 2 == 1) & (np.arange(length) >= 2)
    basis = np.where(is_sine[None, :], np.sin(angles), np.cos(angles))
    scale = np.where(np.arange(length) < 2, 1.0 / length, 2.0 / length)
    return basis.astype(np.float32), (basis.T * scale[:, None]).astype(np.float32)


def widened(table):
    high = table.astype(jnp.bfloat16)
    low = (table - high.astype(np.float32)).astype(jnp.bfloat16)
    return jnp.asarray(np.concatenate([high, high, low], axis=1))


def halves(x):
    high = x.astype(BF16)
    return high, (x - high.astype(F32)).astype(BF16)


def derive(x, first_row, length):
    rows = lax.broadcasted_iota(jnp.int32, x.shape, 0)
    up = pltpu.roll(x, x.shape[0] - 1, 0)
    down = pltpu.roll(x, 1, 0)
    freq = ((rows + first_row) // 2).astype(F32) * (2.0 / length)
    return freq * jnp.where(rows % 2 == 0, up, -down)


def nodal_kernel(length, block, s_ref, g_ref, c_ref, cond_ref, cap_ref, basis_ref, forward_ref, o_ref):
    s_high, s_low = halves(s_ref[...].reshape(length, s_ref.shape[2]))
    waves = jnp.dot(
        basis_ref[...],
        jnp.concatenate([s_high, s_low, s_high], axis=0),
        preferred_element_type=F32,
    )

    def onward(values):
        high, low = halves(values)
        return jnp.dot(
            forward_ref[...],
            jnp.concatenate([high, low, high], axis=0),
            preferred_element_type=F32,
        )

    direct = onward(g_ref[...] * waves)
    stored = onward(c_ref[...] * waves)
    direct_net = []
    stored_net = []
    for b in range(cond_ref.shape[0]):
        cond_high, cond_low = halves(cond_ref[b])
        cap_high, cap_low = halves(cap_ref[b])
        left = jnp.concatenate(
            [
                s_high[:, b * block : (b + 1) * block],
                s_low[:, b * block : (b + 1) * block],
                s_high[:, b * block : (b + 1) * block],
            ],
            axis=1,
        )
        right = jnp.concatenate(
            [
                jnp.concatenate([cond_high, cond_high, cond_low], axis=1),
                jnp.concatenate([cap_high, cap_high, cap_low], axis=1),
            ],
            axis=0,
        )
        both = lax.dot_general(
            left, right, (((1,), (1,)), ((), ())), preferred_element_type=F32
        )
        direct_net.append(both[:, :block])
        stored_net.append(both[:, block:])
    direct = direct + jnp.concatenate(direct_net, axis=1)
    stored = stored + jnp.concatenate(stored_net, axis=1)
    o_ref[...] = (direct + derive(stored, 0, length)).reshape(o_ref.shape)


def nodal(part, s, conductance, capacitance, block_cond, block_cap, basis, forward):
    count, rows, width = s.shape
    length = count * rows
    block = block_cond.shape[1]
    steps = width // TILE
    per = TILE // block
    column = lambda i: (0, part * steps + i)
    blocks = pl.BlockSpec((per, block, block), lambda i: (part * steps + i, 0, 0))
    table = pl.BlockSpec((length, 3 * length), lambda i: (0, 0))
    return pl.pallas_call(
        functools.partial(nodal_kernel, length, block),
        grid=(steps,),
        in_specs=[
            pl.BlockSpec((count, rows, TILE), lambda i: (0, 0, i)),
            pl.BlockSpec((length, TILE), column),
            pl.BlockSpec((length, TILE), column),
            blocks,
            blocks,
            table,
            table,
        ],
        out_specs=pl.BlockSpec((count, rows, TILE), lambda i: (0, 0, i)),
        out_shape=jax.ShapeDtypeStruct(s.shape, F32),
        compiler_params=pltpu.CompilerParams(vmem_limit_bytes=48 << 20),
        cost_estimate=pl.CostEstimate(
            flops=24 * length * length * width, transcendentals=0, bytes_accessed=20 * length * width
        ),
        name="nodal",
    )(in_hbm(s), conductance, capacitance, block_cond, block_cap, basis, forward)


def pack_kernel(offset, stride, x_ref, o_ref, held, sem_in, sem_out):
    count, _, width = o_ref.shape
    loads = [
        pltpu.make_async_copy(
            x_ref.at[:, pl.ds(t * stride + offset, width)], held.at[t], sem_in.at[t]
        )
        for t in range(count)
    ]
    stores = [
        pltpu.make_async_copy(held.at[t], o_ref.at[t], sem_out.at[t]) for t in range(count)
    ]
    for load in loads:
        load.start()
    for load, store in zip(loads, stores):
        load.wait()
        store.start()
    for store in stores:
        store.wait()


def pack(x, part, count):
    rows, columns = x.shape
    stride = columns // count
    width = stride // PARTS
    return pl.pallas_call(
        functools.partial(pack_kernel, part * width, stride),
        in_specs=[pl.BlockSpec(memory_space=pl.ANY)],
        out_specs=pl.BlockSpec(memory_space=pl.ANY),
        out_shape=jax.ShapeDtypeStruct((count, rows, width), F32),
        scratch_shapes=[
            pltpu.VMEM((count, rows, width), F32),
            pltpu.SemaphoreType.DMA((count,)),
            pltpu.SemaphoreType.DMA((count,)),
        ],
        name="pack",
    )(x)


def pick_kernel(per, stride, nodes_ref, x_ref, o_ref):
    group = o_ref.shape[0]
    lanes = lax.broadcasted_iota(jnp.int32, (x_ref.shape[0], 128), 1)
    for g in range(group):
        t = pl.program_id(0) * group + g
        total = jnp.zeros((x_ref.shape[0], 128), F32)
        for j in range(per):
            spot = nodes_ref[t * per + j] + g * stride
            tile = x_ref[:, pl.ds(pl.multiple_of(spot & ~127, 128), 128)]
            turned = pltpu.roll(tile, (j - spot) & 127, 1)
            total = jnp.where(lanes == j, turned, total)
        o_ref[g] = total


def pick(x, nodes, count):
    rows, columns = x.shape
    per = nodes.shape[0] // count
    stride = columns // count
    picked = pl.pallas_call(
        functools.partial(pick_kernel, per, stride),
        grid_spec=pltpu.PrefetchScalarGridSpec(
            num_scalar_prefetch=1,
            grid=(count // GROUP,),
            in_specs=[pl.BlockSpec((rows, GROUP * stride), lambda t, n: (0, t))],
            out_specs=pl.BlockSpec((GROUP, rows, 128), lambda t, n: (t, 0, 0)),
        ),
        out_shape=jax.ShapeDtypeStruct((count, rows, 128), F32),
        name="pick",
    )(nodes, x)
    return picked[:, :, :per].transpose(1, 0, 2).reshape(rows, nodes.shape[0])


def couple_kernel(length, scalars_ref, x_ref, cond_ref, cap_ref, o_ref):
    c = pl.program_id(0)

    @pl.when(c == 0)
    def _():
        o_ref[...] = jnp.zeros_like(o_ref)

    @pl.when(c < scalars_ref[0])
    def _():
        x = x_ref[...]
        slope = derive(x, scalars_ref[1], length)

        def times(left, right):
            left_high, left_low = halves(left)
            right_high, right_low = halves(right)
            contract = (((1,), (1,)), ((), ()))
            product = functools.partial(
                lax.dot_general, dimension_numbers=contract, preferred_element_type=F32
            )
            return (
                product(left_high, right_high)
                + product(left_low, right_high)
                + product(left_high, right_low)
            )

        o_ref[...] += times(x, cond_ref[...]) + times(slope, cap_ref[...])


def couple(gathered, sources, used, first_row, length, couple_cond, couple_cap):
    _, rows, bound = gathered.shape
    slots = sources.shape[0]
    scalars = jnp.concatenate([used, first_row[None], sources])
    table = pl.BlockSpec((None, None, bound, bound), lambda c, n: (0, c, 0, 0))
    return pl.pallas_call(
        functools.partial(couple_kernel, length),
        grid_spec=pltpu.PrefetchScalarGridSpec(
            num_scalar_prefetch=1,
            grid=(slots,),
            in_specs=[
                pl.BlockSpec((None, rows, bound), lambda c, n: (n[2 + c], 0, 0)),
                table,
                table,
            ],
            out_specs=pl.BlockSpec((rows, bound), lambda c, n: (0, 0)),
        ),
        out_shape=jax.ShapeDtypeStruct((rows, bound), F32),
        name="couple",
    )(scalars, gathered, couple_cond, couple_cap)


def spread_kernel(stride, nodes_ref, extra_ref, o_ref):
    group, rows, per = extra_ref.shape
    lanes = lax.broadcasted_iota(jnp.int32, (rows, 128), 1)
    o_ref[...] = jnp.zeros_like(o_ref)
    for g in range(group):
        t = pl.program_id(0) * group + g
        extra = extra_ref[g]
        for j in range(per):
            spot = nodes_ref[t * per + j] + g * stride
            at = pl.ds(pl.multiple_of(spot & ~127, 128), 128)
            o_ref[:, at] += jnp.where(lanes == (spot & 127), extra[:, j : j + 1], 0.0)


def spread(extra, nodes, stride):
    count, rows, per = extra.shape
    return pl.pallas_call(
        functools.partial(spread_kernel, stride),
        grid_spec=pltpu.PrefetchScalarGridSpec(
            num_scalar_prefetch=1,
            grid=(count // GROUP,),
            in_specs=[pl.BlockSpec((GROUP, rows, per), lambda t, n: (t, 0, 0))],
            out_specs=pl.BlockSpec((rows, GROUP * stride), lambda t, n: (0, t)),
        ),
        out_shape=jax.ShapeDtypeStruct((rows, count * stride), F32),
        name="spread",
    )(nodes, extra)


def place_kernel(*refs):
    y_refs, held_ref, o_ref = refs[:PARTS], refs[PARTS], refs[PARTS + 1]
    y_buf, held_buf, sem_y, sem_held, sem_out = refs[PARTS + 2 :]
    count, _, width = y_refs[0].shape
    at = [pl.ds(t * width * PARTS, width * PARTS) for t in range(count)]
    loads = [
        [pltpu.make_async_copy(held_ref.at[:, at[t]], held_buf.at[t], sem_held.at[t])]
        + [
            pltpu.make_async_copy(
                y_refs[p].at[t], y_buf.at[t, :, pl.ds(p * width, width)], sem_y.at[p, t]
            )
            for p in range(PARTS)
        ]
        for t in range(count)
    ]
    stores = [
        pltpu.make_async_copy(y_buf.at[t], o_ref.at[:, at[t]], sem_out.at[t])
        for t in range(count)
    ]
    for group in loads:
        for load in group:
            load.start()
    for t in range(count):
        for load in loads[t]:
            load.wait()
        y_buf[t] = y_buf[t] + held_buf[t]
        stores[t].start()
    for store in stores:
        store.wait()


def place(ys, held):
    count, rows, width = ys[0].shape
    whole = (count, rows, width * PARTS)
    return pl.pallas_call(
        place_kernel,
        in_specs=[pl.BlockSpec(memory_space=pl.ANY)] * (PARTS + 1),
        out_specs=pl.BlockSpec(memory_space=pl.ANY),
        out_shape=jax.ShapeDtypeStruct(held.shape, F32),
        scratch_shapes=[
            pltpu.VMEM(whole, F32),
            pltpu.VMEM(whole, F32),
            pltpu.SemaphoreType.DMA((PARTS, count)),
            pltpu.SemaphoreType.DMA((count,)),
            pltpu.SemaphoreType.DMA((count,)),
        ],
        compiler_params=pltpu.CompilerParams(vmem_limit_bytes=48 << 20),
        name="place",
    )(*[in_hbm(y) for y in ys], held)


def in_hbm(x):
    return pltpu.with_memory_space_constraint(x, pltpu.HBM)


def shards(
    spectrum,
    conductance,
    capacitance,
    block_cond,
    block_cap,
    boundary_nodes,
    couple_src,
    couple_count,
    couple_cond,
    couple_cap,
):
    length = conductance.shape[0]
    rows = spectrum.shape[0]
    count = lax.axis_size("spec")
    doms = lax.axis_size("dom")
    basis_table, forward_table = fourier_tables(length)
    basis, forward = widened(basis_table), widened(forward_table)
    stride = spectrum.shape[1] // count
    nodes = boundary_nodes[0]
    slices = jnp.arange(nodes.shape[0], dtype=jnp.int32) // (nodes.shape[0] // count)
    nodes = jnp.clip(nodes - slices * stride, 0, stride - 1)
    nodal_args = (conductance, capacitance, block_cond, block_cap, basis, forward)

    def swap(x):
        return lax.all_to_all(x, "spec", split_axis=0, concat_axis=0, tiled=True)

    arrived = []
    for part in range(PARTS):
        packed = pack(spectrum, part, count)
        if part == 1:
            own_boundary = pick(spectrum, nodes, count)
            moved = [
                lax.ppermute(own_boundary, "dom", [(d, (d + k) % doms) for d in range(doms)])
                for k in range(1, doms)
            ]
            packed, moved[:EARLY] = lax.optimization_barrier((packed, moved[:EARLY]))
        arrived.append(swap(packed))

    current = nodal(0, arrived[0], *nodal_args)
    current, moved = lax.optimization_barrier((current, moved))
    first = swap(current)

    extra = couple(
        jnp.stack(moved),
        (lax.axis_index("dom") - couple_src[0]) % doms - 1,
        couple_count,
        lax.axis_index("spec") * rows,
        length,
        couple_cond,
        couple_cap,
    )
    extra = extra.reshape(rows, count, nodes.shape[0] // count).transpose(1, 0, 2)

    held = spread(extra, nodes, stride)
    current = nodal(1, arrived[1], *nodal_args)
    current, held = lax.optimization_barrier((current, held))
    return place([first, swap(current)], held)


def solution(mesh):
    return jax.shard_map(
        shards,
        mesh=mesh,
        in_specs=(
            P("spec", "dom"),
            P(None, ("dom", "spec")),
            P(None, ("dom", "spec")),
            P(("dom", "spec"), None, None),
            P(("dom", "spec"), None, None),
            P("dom", None),
            P("dom", None),
            P("dom"),
            P("dom", None, None, None),
            P("dom", None, None, None),
        ),
        out_specs=P("spec", "dom"),
        check_vma=False,
    )
```

```python
import functools
import math

import jax
import jax.numpy as jnp
import numpy as np
from jax import lax
from jax.experimental import pallas as pl
from jax.experimental.pallas import tpu as pltpu
from jax.sharding import PartitionSpec as P

F32 = jnp.float32
BF16 = jnp.bfloat16
SHARES = (5, 3)
TILE = 512
GROUP = 8


def fourier_tables(length):
    harmonic = np.arange(length) // 2
    harmonic[1] = length // 2
    phase = np.arange(length)[:, None] * harmonic[None, :] % length
    angles = phase * (2.0 * math.pi / length)
    is_sine = (np.arange(length) % 2 == 1) & (np.arange(length) >= 2)
    basis = np.where(is_sine[None, :], np.sin(angles), np.cos(angles))
    scale = np.where(np.arange(length) < 2, 1.0 / length, 2.0 / length)
    return basis.astype(np.float32), (basis.T * scale[:, None]).astype(np.float32)


def widened(table):
    high = table.astype(jnp.bfloat16)
    low = (table - high.astype(np.float32)).astype(jnp.bfloat16)
    return jnp.asarray(np.concatenate([high, high, low], axis=1))


def halves(x):
    high = x.astype(BF16)
    return high, (x - high.astype(F32)).astype(BF16)


def derive(x, first_row, length):
    rows = lax.broadcasted_iota(jnp.int32, x.shape, 0)
    up = pltpu.roll(x, x.shape[0] - 1, 0)
    down = pltpu.roll(x, 1, 0)
    freq = ((rows + first_row) // 2).astype(F32) * (2.0 / length)
    return freq * jnp.where(rows % 2 == 0, up, -down)


def nodal_kernel(length, block, s_ref, g_ref, c_ref, cond_ref, cap_ref, basis_ref, forward_ref, *rest):
    o_ref = rest[-1]
    s_high, s_low = halves(s_ref[...].reshape(length, s_ref.shape[2]))
    waves = jnp.dot(
        basis_ref[...],
        jnp.concatenate([s_high, s_low, s_high], axis=0),
        preferred_element_type=F32,
    )

    def onward(values):
        high, low = halves(values)
        return jnp.dot(
            forward_ref[...],
            jnp.concatenate([high, low, high], axis=0),
            preferred_element_type=F32,
        )

    direct = onward(g_ref[...] * waves)
    stored = onward(c_ref[...] * waves)
    direct_net = []
    stored_net = []
    for b in range(cond_ref.shape[0]):
        cond_high, cond_low = halves(cond_ref[b])
        cap_high, cap_low = halves(cap_ref[b])
        left = jnp.concatenate(
            [
                s_high[:, b * block : (b + 1) * block],
                s_low[:, b * block : (b + 1) * block],
                s_high[:, b * block : (b + 1) * block],
            ],
            axis=1,
        )
        right = jnp.concatenate(
            [
                jnp.concatenate([cond_high, cond_high, cond_low], axis=1),
                jnp.concatenate([cap_high, cap_high, cap_low], axis=1),
            ],
            axis=0,
        )
        both = lax.dot_general(
            left, right, (((1,), (1,)), ((), ())), preferred_element_type=F32
        )
        direct_net.append(both[:, :block])
        stored_net.append(both[:, block:])
    direct = direct + jnp.concatenate(direct_net, axis=1)
    stored = stored + jnp.concatenate(stored_net, axis=1)
    o_ref[...] = (direct + derive(stored, 0, length)).reshape(o_ref.shape)


def nodal(first, held, s, conductance, capacitance, block_cond, block_cap, basis, forward):
    count, rows, width = s.shape
    length = count * rows
    block = block_cond.shape[1]
    steps = width // TILE
    per = TILE // block
    column = lambda i: (0, first + i)
    blocks = pl.BlockSpec((per, block, block), lambda i: (first + i, 0, 0))
    table = pl.BlockSpec((length, 3 * length), lambda i: (0, 0))
    more = [] if held is None else [held]
    return pl.pallas_call(
        functools.partial(nodal_kernel, length, block),
        grid=(steps,),
        in_specs=[
            pl.BlockSpec((count, rows, TILE), lambda i: (0, 0, i)),
            pl.BlockSpec((length, TILE), column),
            pl.BlockSpec((length, TILE), column),
            blocks,
            blocks,
            table,
            table,
        ]
        + [pl.BlockSpec(memory_space=pl.ANY)] * len(more),
        out_specs=pl.BlockSpec((count, rows, TILE), lambda i: (0, 0, first + i)),
        out_shape=jax.ShapeDtypeStruct((count, rows, conductance.shape[1]), F32),
        input_output_aliases={7: 0} if more else {},
        compiler_params=pltpu.CompilerParams(vmem_limit_bytes=48 << 20),
        cost_estimate=pl.CostEstimate(
            flops=24 * length * length * width, transcendentals=0, bytes_accessed=20 * length * width
        ),
        name="nodal",
    )(in_hbm(s), conductance, capacitance, block_cond, block_cap, basis, forward, *more)


def pack_kernel(offset, stride, x_ref, o_ref, held, sem_in, sem_out):
    count, _, width = o_ref.shape
    loads = [
        pltpu.make_async_copy(
            x_ref.at[:, pl.ds(t * stride + offset, width)], held.at[t], sem_in.at[t]
        )
        for t in range(count)
    ]
    stores = [
        pltpu.make_async_copy(held.at[t], o_ref.at[t], sem_out.at[t]) for t in range(count)
    ]
    for load in loads:
        load.start()
    for load, store in zip(loads, stores):
        load.wait()
        store.start()
    for store in stores:
        store.wait()


def pack(x, offset, width, count):
    rows, columns = x.shape
    stride = columns // count
    return pl.pallas_call(
        functools.partial(pack_kernel, offset, stride),
        in_specs=[pl.BlockSpec(memory_space=pl.ANY)],
        out_specs=pl.BlockSpec(memory_space=pl.ANY),
        out_shape=jax.ShapeDtypeStruct((count, rows, width), F32),
        scratch_shapes=[
            pltpu.VMEM((count, rows, width), F32),
            pltpu.SemaphoreType.DMA((count,)),
            pltpu.SemaphoreType.DMA((count,)),
        ],
        name="pack",
    )(x)


def pick_kernel(per, stride, nodes_ref, x_ref, o_ref):
    group = o_ref.shape[0]
    lanes = lax.broadcasted_iota(jnp.int32, (x_ref.shape[0], 128), 1)
    for g in range(group):
        t = pl.program_id(0) * group + g
        total = jnp.zeros((x_ref.shape[0], 128), F32)
        for j in range(per):
            spot = nodes_ref[t * per + j] + g * stride
            tile = x_ref[:, pl.ds(pl.multiple_of(spot & ~127, 128), 128)]
            turned = pltpu.roll(tile, (j - spot) & 127, 1)
            total = jnp.where(lanes == j, turned, total)
        o_ref[g] = total


def pick(x, nodes, count):
    rows, columns = x.shape
    per = nodes.shape[0] // count
    stride = columns // count
    picked = pl.pallas_call(
        functools.partial(pick_kernel, per, stride),
        grid_spec=pltpu.PrefetchScalarGridSpec(
            num_scalar_prefetch=1,
            grid=(count // GROUP,),
            in_specs=[pl.BlockSpec((rows, GROUP * stride), lambda t, n: (0, t))],
            out_specs=pl.BlockSpec((GROUP, rows, 128), lambda t, n: (t, 0, 0)),
        ),
        out_shape=jax.ShapeDtypeStruct((count, rows, 128), F32),
        name="pick",
    )(nodes, x)
    return picked[:, :, :per].transpose(1, 0, 2).reshape(rows, nodes.shape[0])


def couple_kernel(length, scalars_ref, x_ref, cond_ref, cap_ref, o_ref):
    c = pl.program_id(0)

    @pl.when(c == 0)
    def _():
        o_ref[...] = jnp.zeros_like(o_ref)

    @pl.when(c < scalars_ref[0])
    def _():
        x = x_ref[...]
        slope = derive(x, scalars_ref[1], length)

        def times(left, right):
            left_high, left_low = halves(left)
            right_high, right_low = halves(right)
            contract = (((1,), (1,)), ((), ()))
            product = functools.partial(
                lax.dot_general, dimension_numbers=contract, preferred_element_type=F32
            )
            return (
                product(left_high, right_high)
                + product(left_low, right_high)
                + product(left_high, right_low)
            )

        o_ref[...] += times(x, cond_ref[...]) + times(slope, cap_ref[...])


def couple(gathered, sources, used, first_row, length, couple_cond, couple_cap):
    _, rows, bound = gathered.shape
    slots = sources.shape[0]
    scalars = jnp.concatenate([used, first_row[None], sources])
    table = pl.BlockSpec((None, None, bound, bound), lambda c, n: (0, c, 0, 0))
    return pl.pallas_call(
        functools.partial(couple_kernel, length),
        grid_spec=pltpu.PrefetchScalarGridSpec(
            num_scalar_prefetch=1,
            grid=(slots,),
            in_specs=[
                pl.BlockSpec((None, rows, bound), lambda c, n: (n[2 + c], 0, 0)),
                table,
                table,
            ],
            out_specs=pl.BlockSpec((rows, bound), lambda c, n: (0, 0)),
        ),
        out_shape=jax.ShapeDtypeStruct((rows, bound), F32),
        name="couple",
    )(scalars, gathered, couple_cond, couple_cap)


def spread_kernel(stride, nodes_ref, extra_ref, o_ref):
    group, rows, per = extra_ref.shape
    lanes = lax.broadcasted_iota(jnp.int32, (rows, 128), 1)
    o_ref[...] = jnp.zeros_like(o_ref)
    for g in range(group):
        t = pl.program_id(0) * group + g
        extra = extra_ref[g]
        for j in range(per):
            spot = nodes_ref[t * per + j] + g * stride
            at = pl.ds(pl.multiple_of(spot & ~127, 128), 128)
            o_ref[:, at] += jnp.where(lanes == (spot & 127), extra[:, j : j + 1], 0.0)


def spread(extra, nodes, stride):
    count, rows, per = extra.shape
    return pl.pallas_call(
        functools.partial(spread_kernel, stride),
        grid_spec=pltpu.PrefetchScalarGridSpec(
            num_scalar_prefetch=1,
            grid=(count // GROUP,),
            in_specs=[pl.BlockSpec((GROUP, rows, per), lambda t, n: (t, 0, 0))],
            out_specs=pl.BlockSpec((rows, GROUP * stride), lambda t, n: (0, t)),
        ),
        out_shape=jax.ShapeDtypeStruct((rows, count * stride), F32),
        name="spread",
    )(nodes, extra)


def place_kernel(y_ref, held_ref, o_ref, y_buf, held_buf, sem_y, sem_held, sem_out):
    count, _, stride = y_ref.shape
    at = [pl.ds(t * stride, stride) for t in range(count)]
    loads = [
        (
            pltpu.make_async_copy(y_ref.at[t], y_buf.at[t], sem_y.at[t]),
            pltpu.make_async_copy(held_ref.at[:, at[t]], held_buf.at[t], sem_held.at[t]),
        )
        for t in range(count)
    ]
    stores = [
        pltpu.make_async_copy(y_buf.at[t], o_ref.at[:, at[t]], sem_out.at[t])
        for t in range(count)
    ]
    for first, second in loads:
        first.start()
        second.start()
    for t in range(count):
        loads[t][0].wait()
        loads[t][1].wait()
        y_buf[t] = y_buf[t] + held_buf[t]
        stores[t].start()
    for store in stores:
        store.wait()


def place(y, held):
    count = y.shape[0]
    return pl.pallas_call(
        place_kernel,
        in_specs=[pl.BlockSpec(memory_space=pl.ANY)] * 2,
        out_specs=pl.BlockSpec(memory_space=pl.ANY),
        out_shape=jax.ShapeDtypeStruct(held.shape, F32),
        scratch_shapes=[
            pltpu.VMEM(y.shape, F32),
            pltpu.VMEM(y.shape, F32),
            pltpu.SemaphoreType.DMA((count,)),
            pltpu.SemaphoreType.DMA((count,)),
            pltpu.SemaphoreType.DMA((count,)),
        ],
        compiler_params=pltpu.CompilerParams(vmem_limit_bytes=48 << 20),
        name="place",
    )(in_hbm(y), held)


def in_hbm(x):
    return pltpu.with_memory_space_constraint(x, pltpu.HBM)


def shards(
    spectrum,
    conductance,
    capacitance,
    block_cond,
    block_cap,
    boundary_nodes,
    couple_src,
    couple_count,
    couple_cond,
    couple_cap,
):
    length = conductance.shape[0]
    rows = spectrum.shape[0]
    count = lax.axis_size("spec")
    doms = lax.axis_size("dom")
    basis_table, forward_table = fourier_tables(length)
    basis, forward = widened(basis_table), widened(forward_table)
    stride = spectrum.shape[1] // count
    nodes = boundary_nodes[0]
    slices = jnp.arange(nodes.shape[0], dtype=jnp.int32) // (nodes.shape[0] // count)
    nodes = jnp.clip(nodes - slices * stride, 0, stride - 1)
    nodal_args = (conductance, capacitance, block_cond, block_cap, basis, forward)

    def swap(x):
        return lax.all_to_all(x, "spec", split_axis=0, concat_axis=0, tiled=True)

    tiles = stride // TILE
    early = tiles * SHARES[0] // sum(SHARES)
    first = swap(pack(spectrum, 0, early * TILE, count))

    own_boundary = pick(spectrum, nodes, count)
    moved = [
        lax.ppermute(own_boundary, "dom", [(d, (d + k) % doms) for d in range(doms)])
        for k in range(1, doms)
    ]
    packed = pack(spectrum, early * TILE, (tiles - early) * TILE, count)
    extra = couple(
        jnp.stack(moved),
        (lax.axis_index("dom") - couple_src[0]) % doms - 1,
        couple_count,
        lax.axis_index("spec") * rows,
        length,
        couple_cond,
        couple_cap,
    )
    extra = extra.reshape(rows, count, nodes.shape[0] // count).transpose(1, 0, 2)

    packed, extra, first = lax.optimization_barrier((packed, extra, first))
    second = swap(packed)
    held = spread(extra, nodes, stride)
    second, held = lax.optimization_barrier((second, held))

    current = nodal(0, None, first, *nodal_args)
    current = nodal(early, current, second, *nodal_args)
    back = swap(current)

    return place(back, held)


def solution(mesh):
    return jax.shard_map(
        shards,
        mesh=mesh,
        in_specs=(
            P("spec", "dom"),
            P(None, ("dom", "spec")),
            P(None, ("dom", "spec")),
            P(("dom", "spec"), None, None),
            P(("dom", "spec"), None, None),
            P("dom", None),
            P("dom", None),
            P("dom"),
            P("dom", None, None, None),
            P("dom", None, None, None),
        ),
        out_specs=P("spec", "dom"),
        check_vma=False,
    )
```

```python
import functools
import math

import jax
import jax.numpy as jnp
import numpy as np
from jax import lax
from jax.experimental import pallas as pl
from jax.experimental.pallas import tpu as pltpu
from jax.sharding import PartitionSpec as P

F32 = jnp.float32
BF16 = jnp.bfloat16
SHARES = (5, 3)
TILE = 256
GROUP = 8


def fourier_tables(length):
    harmonic = np.arange(length) // 2
    harmonic[1] = length // 2
    phase = np.arange(length)[:, None] * harmonic[None, :] % length
    angles = phase * (2.0 * math.pi / length)
    is_sine = (np.arange(length) % 2 == 1) & (np.arange(length) >= 2)
    basis = np.where(is_sine[None, :], np.sin(angles), np.cos(angles))
    scale = np.where(np.arange(length) < 2, 1.0 / length, 2.0 / length)
    return basis.astype(np.float32), (basis.T * scale[:, None]).astype(np.float32)


def widened(table):
    high = table.astype(jnp.bfloat16)
    low = (table - high.astype(np.float32)).astype(jnp.bfloat16)
    return jnp.asarray(np.concatenate([high, high, low], axis=1))


def halves(x):
    high = x.astype(BF16)
    return high, (x - high.astype(F32)).astype(BF16)


def derive(x, first_row, length):
    rows = lax.broadcasted_iota(jnp.int32, x.shape, 0)
    up = pltpu.roll(x, x.shape[0] - 1, 0)
    down = pltpu.roll(x, 1, 0)
    freq = ((rows + first_row) // 2).astype(F32) * (2.0 / length)
    return freq * jnp.where(rows % 2 == 0, up, -down)


def nodal_kernel(length, block, s_ref, g_ref, c_ref, cond_ref, cap_ref, basis_ref, forward_ref, *rest):
    o_ref = rest[-1]
    s_high, s_low = halves(s_ref[...].reshape(length, s_ref.shape[2]))
    waves = jnp.dot(
        basis_ref[...],
        jnp.concatenate([s_high, s_low, s_high], axis=0),
        preferred_element_type=F32,
    )

    def onward(values):
        high, low = halves(values)
        return jnp.dot(
            forward_ref[...],
            jnp.concatenate([high, low, high], axis=0),
            preferred_element_type=F32,
        )

    direct = onward(g_ref[...] * waves)
    stored = onward(c_ref[...] * waves)
    direct_net = []
    stored_net = []
    for b in range(cond_ref.shape[0]):
        cond_high, cond_low = halves(cond_ref[b])
        cap_high, cap_low = halves(cap_ref[b])
        left = jnp.concatenate(
            [
                s_high[:, b * block : (b + 1) * block],
                s_low[:, b * block : (b + 1) * block],
                s_high[:, b * block : (b + 1) * block],
            ],
            axis=1,
        )
        right = jnp.concatenate(
            [
                jnp.concatenate([cond_high, cond_high, cond_low], axis=1),
                jnp.concatenate([cap_high, cap_high, cap_low], axis=1),
            ],
            axis=0,
        )
        both = lax.dot_general(
            left, right, (((1,), (1,)), ((), ())), preferred_element_type=F32
        )
        direct_net.append(both[:, :block])
        stored_net.append(both[:, block:])
    direct = direct + jnp.concatenate(direct_net, axis=1)
    stored = stored + jnp.concatenate(stored_net, axis=1)
    o_ref[...] = (direct + derive(stored, 0, length)).reshape(o_ref.shape)


def nodal(first, held, s, conductance, capacitance, block_cond, block_cap, basis, forward):
    count, rows, width = s.shape
    length = count * rows
    block = block_cond.shape[1]
    steps = width // TILE
    per = TILE // block
    column = lambda i: (0, first + i)
    blocks = pl.BlockSpec((per, block, block), lambda i: (first + i, 0, 0))
    table = pl.BlockSpec((length, 3 * length), lambda i: (0, 0))
    more = [] if held is None else [held]
    return pl.pallas_call(
        functools.partial(nodal_kernel, length, block),
        grid=(steps,),
        in_specs=[
            pl.BlockSpec((count, rows, TILE), lambda i: (0, 0, i)),
            pl.BlockSpec((length, TILE), column),
            pl.BlockSpec((length, TILE), column),
            blocks,
            blocks,
            table,
            table,
        ]
        + [pl.BlockSpec(memory_space=pl.ANY)] * len(more),
        out_specs=pl.BlockSpec((count, rows, TILE), lambda i: (0, 0, first + i)),
        out_shape=jax.ShapeDtypeStruct((count, rows, conductance.shape[1]), F32),
        input_output_aliases={7: 0} if more else {},
        compiler_params=pltpu.CompilerParams(vmem_limit_bytes=48 << 20),
        cost_estimate=pl.CostEstimate(
            flops=24 * length * length * width, transcendentals=0, bytes_accessed=20 * length * width
        ),
        name="nodal",
    )(in_hbm(s), conductance, capacitance, block_cond, block_cap, basis, forward, *more)


def pack_kernel(offset, stride, x_ref, o_ref, held, sem_in, sem_out):
    count, _, width = o_ref.shape
    loads = [
        pltpu.make_async_copy(
            x_ref.at[:, pl.ds(t * stride + offset, width)], held.at[t], sem_in.at[t]
        )
        for t in range(count)
    ]
    stores = [
        pltpu.make_async_copy(held.at[t], o_ref.at[t], sem_out.at[t]) for t in range(count)
    ]
    for load in loads:
        load.start()
    for load, store in zip(loads, stores):
        load.wait()
        store.start()
    for store in stores:
        store.wait()


def pack(x, offset, width, count):
    rows, columns = x.shape
    stride = columns // count
    return pl.pallas_call(
        functools.partial(pack_kernel, offset, stride),
        in_specs=[pl.BlockSpec(memory_space=pl.ANY)],
        out_specs=pl.BlockSpec(memory_space=pl.ANY),
        out_shape=jax.ShapeDtypeStruct((count, rows, width), F32),
        scratch_shapes=[
            pltpu.VMEM((count, rows, width), F32),
            pltpu.SemaphoreType.DMA((count,)),
            pltpu.SemaphoreType.DMA((count,)),
        ],
        name="pack",
    )(x)


def pick_kernel(per, stride, nodes_ref, x_ref, o_ref):
    group = o_ref.shape[0]
    lanes = lax.broadcasted_iota(jnp.int32, (x_ref.shape[0], 128), 1)
    for g in range(group):
        t = pl.program_id(0) * group + g
        total = jnp.zeros((x_ref.shape[0], 128), F32)
        for j in range(per):
            spot = nodes_ref[t * per + j] + g * stride
            tile = x_ref[:, pl.ds(pl.multiple_of(spot & ~127, 128), 128)]
            turned = pltpu.roll(tile, (j - spot) & 127, 1)
            total = jnp.where(lanes == j, turned, total)
        o_ref[g] = total


def pick(x, nodes, count):
    rows, columns = x.shape
    per = nodes.shape[0] // count
    stride = columns // count
    picked = pl.pallas_call(
        functools.partial(pick_kernel, per, stride),
        grid_spec=pltpu.PrefetchScalarGridSpec(
            num_scalar_prefetch=1,
            grid=(count // GROUP,),
            in_specs=[pl.BlockSpec((rows, GROUP * stride), lambda t, n: (0, t))],
            out_specs=pl.BlockSpec((GROUP, rows, 128), lambda t, n: (t, 0, 0)),
        ),
        out_shape=jax.ShapeDtypeStruct((count, rows, 128), F32),
        name="pick",
    )(nodes, x)
    return picked[:, :, :per].transpose(1, 0, 2).reshape(rows, nodes.shape[0])


def couple_kernel(length, scalars_ref, x_ref, cond_ref, cap_ref, o_ref):
    c = pl.program_id(0)

    @pl.when(c == 0)
    def _():
        o_ref[...] = jnp.zeros_like(o_ref)

    @pl.when(c < scalars_ref[0])
    def _():
        x = x_ref[...]
        slope = derive(x, scalars_ref[1], length)

        def times(left, right):
            left_high, left_low = halves(left)
            right_high, right_low = halves(right)
            contract = (((1,), (1,)), ((), ()))
            product = functools.partial(
                lax.dot_general, dimension_numbers=contract, preferred_element_type=F32
            )
            return (
                product(left_high, right_high)
                + product(left_low, right_high)
                + product(left_high, right_low)
            )

        o_ref[...] += times(x, cond_ref[...]) + times(slope, cap_ref[...])


def couple(gathered, sources, used, first_row, length, couple_cond, couple_cap):
    _, rows, bound = gathered.shape
    slots = sources.shape[0]
    scalars = jnp.concatenate([used, first_row[None], sources])
    table = pl.BlockSpec((None, None, bound, bound), lambda c, n: (0, c, 0, 0))
    return pl.pallas_call(
        functools.partial(couple_kernel, length),
        grid_spec=pltpu.PrefetchScalarGridSpec(
            num_scalar_prefetch=1,
            grid=(slots,),
            in_specs=[
                pl.BlockSpec((None, rows, bound), lambda c, n: (n[2 + c], 0, 0)),
                table,
                table,
            ],
            out_specs=pl.BlockSpec((rows, bound), lambda c, n: (0, 0)),
        ),
        out_shape=jax.ShapeDtypeStruct((rows, bound), F32),
        name="couple",
    )(scalars, gathered, couple_cond, couple_cap)


def spread_kernel(stride, nodes_ref, extra_ref, o_ref):
    group, rows, per = extra_ref.shape
    lanes = lax.broadcasted_iota(jnp.int32, (rows, 128), 1)
    o_ref[...] = jnp.zeros_like(o_ref)
    for g in range(group):
        t = pl.program_id(0) * group + g
        extra = extra_ref[g]
        for j in range(per):
            spot = nodes_ref[t * per + j] + g * stride
            at = pl.ds(pl.multiple_of(spot & ~127, 128), 128)
            o_ref[:, at] += jnp.where(lanes == (spot & 127), extra[:, j : j + 1], 0.0)


def spread(extra, nodes, stride):
    count, rows, per = extra.shape
    return pl.pallas_call(
        functools.partial(spread_kernel, stride),
        grid_spec=pltpu.PrefetchScalarGridSpec(
            num_scalar_prefetch=1,
            grid=(count // GROUP,),
            in_specs=[pl.BlockSpec((GROUP, rows, per), lambda t, n: (t, 0, 0))],
            out_specs=pl.BlockSpec((rows, GROUP * stride), lambda t, n: (0, t)),
        ),
        out_shape=jax.ShapeDtypeStruct((rows, count * stride), F32),
        name="spread",
    )(nodes, extra)


def place_kernel(y_ref, held_ref, o_ref, y_buf, held_buf, sem_y, sem_held, sem_out):
    count, _, stride = y_ref.shape
    at = [pl.ds(t * stride, stride) for t in range(count)]
    loads = [
        (
            pltpu.make_async_copy(y_ref.at[t], y_buf.at[t], sem_y.at[t]),
            pltpu.make_async_copy(held_ref.at[:, at[t]], held_buf.at[t], sem_held.at[t]),
        )
        for t in range(count)
    ]
    stores = [
        pltpu.make_async_copy(y_buf.at[t], o_ref.at[:, at[t]], sem_out.at[t])
        for t in range(count)
    ]
    for first, second in loads:
        first.start()
        second.start()
    for t in range(count):
        loads[t][0].wait()
        loads[t][1].wait()
        y_buf[t] = y_buf[t] + held_buf[t]
        stores[t].start()
    for store in stores:
        store.wait()


def place(y, held):
    count = y.shape[0]
    return pl.pallas_call(
        place_kernel,
        in_specs=[pl.BlockSpec(memory_space=pl.ANY)] * 2,
        out_specs=pl.BlockSpec(memory_space=pl.ANY),
        out_shape=jax.ShapeDtypeStruct(held.shape, F32),
        scratch_shapes=[
            pltpu.VMEM(y.shape, F32),
            pltpu.VMEM(y.shape, F32),
            pltpu.SemaphoreType.DMA((count,)),
            pltpu.SemaphoreType.DMA((count,)),
            pltpu.SemaphoreType.DMA((count,)),
        ],
        compiler_params=pltpu.CompilerParams(vmem_limit_bytes=48 << 20),
        name="place",
    )(in_hbm(y), held)


def in_hbm(x):
    return pltpu.with_memory_space_constraint(x, pltpu.HBM)


def shards(
    spectrum,
    conductance,
    capacitance,
    block_cond,
    block_cap,
    boundary_nodes,
    couple_src,
    couple_count,
    couple_cond,
    couple_cap,
):
    length = conductance.shape[0]
    rows = spectrum.shape[0]
    count = lax.axis_size("spec")
    doms = lax.axis_size("dom")
    basis_table, forward_table = fourier_tables(length)
    basis, forward = widened(basis_table), widened(forward_table)
    stride = spectrum.shape[1] // count
    nodes = boundary_nodes[0]
    slices = jnp.arange(nodes.shape[0], dtype=jnp.int32) // (nodes.shape[0] // count)
    nodes = jnp.clip(nodes - slices * stride, 0, stride - 1)
    nodal_args = (conductance, capacitance, block_cond, block_cap, basis, forward)

    def swap(x):
        return lax.all_to_all(x, "spec", split_axis=0, concat_axis=0, tiled=True)

    tiles = stride // TILE
    early = tiles * SHARES[0] // sum(SHARES)
    first = swap(pack(spectrum, 0, early * TILE, count))

    own_boundary = pick(spectrum, nodes, count)
    moved = [
        lax.ppermute(own_boundary, "dom", [(d, (d + k) % doms) for d in range(doms)])
        for k in range(1, doms)
    ]
    packed = pack(spectrum, early * TILE, (tiles - early) * TILE, count)
    extra = couple(
        jnp.stack(moved),
        (lax.axis_index("dom") - couple_src[0]) % doms - 1,
        couple_count,
        lax.axis_index("spec") * rows,
        length,
        couple_cond,
        couple_cap,
    )
    extra = extra.reshape(rows, count, nodes.shape[0] // count).transpose(1, 0, 2)

    packed, extra, first = lax.optimization_barrier((packed, extra, first))
    second = swap(packed)
    held = spread(extra, nodes, stride)
    second, held = lax.optimization_barrier((second, held))

    current = nodal(0, None, first, *nodal_args)
    current = nodal(early, current, second, *nodal_args)
    back = swap(current)

    return place(back, held)


def solution(mesh):
    return jax.shard_map(
        shards,
        mesh=mesh,
        in_specs=(
            P("spec", "dom"),
            P(None, ("dom", "spec")),
            P(None, ("dom", "spec")),
            P(("dom", "spec"), None, None),
            P(("dom", "spec"), None, None),
            P("dom", None),
            P("dom", None),
            P("dom"),
            P("dom", None, None, None),
            P("dom", None, None, None),
        ),
        out_specs=P("spec", "dom"),
        check_vma=False,
    )
```
